32 devices in a mesh: doc: 4 (over z), seq: 8 (over y, x, core).
Axes of the slice: x: 2, y: 2, z: 4, core: 2. Of those that a mesh axis runs over, the one named last changes fastest.
Arguments:
- features: bfloat16 [4096, 1280], P(('doc', 'seq')), parts along dimension 0, may hold values from -6 to 6
- gate_in: bfloat16 [4096, 1024], P(('doc', 'seq')), parts along dimension 0, may hold values from -6 to 6
- conv_weight: float32 [4, 1280], replicated, may hold values from -3 to 3
- conv_bias: float32 [1280], replicated, may hold values from -0.5 to 0.5
- log_decay: float32 [4096, 16], P(('doc', 'seq')), parts along dimension 0, may hold values from -0.6 to 0
- step_size: float32 [4096, 16], P(('doc', 'seq')), parts along dimension 0, may hold values from 0 to 2
- gate_gain: float32 [1024], replicated, may hold values from 0.25 to 1.75
- w_out: bfloat16 [1024, 1024], replicated, may hold values from -0.1875 to 0.1875
- boundaries: int32 [1024], P('doc'), parts along dimension 0, may hold values from 0 to 1023, as said below
- pad_vector: bfloat16 [512], replicated, may hold values from -5 to 5
- main_gain: float32 [1536], replicated, may hold values from 0.25 to 1.75
- w_gate: bfloat16 [1536, 4096], P(None, 'seq'), may hold values from -0.15625 to 0.15625
- w_up: bfloat16 [1536, 4096], P(None, 'seq'), may hold values from -0.15625 to 0.15625
- w_down: bfloat16 [4096, 1024], P('seq'), may hold values from -0.09375 to 0.09375
Outputs:
- byte_out: bfloat16 [4096, 1024], P(('doc', 'seq')), parts along dimension 0
The draws below stay inside these ranges and needn't reach their ends.
There are 4 independent parts, one for each index of `doc`. The reference program is written for one: setup_inputs(seed, part) draws one part's arguments, and reference() takes and returns one part's arrays. A program takes and returns all parts, laid end to end along the dimension named above; an argument that names none is the same for every part. Nothing has to cross between parts.
Inputs may be any that keep to these rules, and one draw needn't show every extreme that they name: Strictly increasing, boundaries[0] = 0. For every k = 1, 2, ..., the number of entries below k * 128 lies between k * 32 and k * 32 + 31, and the upper end is reached at some k in every draw. The bytes of one device hold 1 to 63 entries, and some device holds exactly 63.
All inputs are finite; a program needn't handle non-finite values.
Results may differ from the reference program's by a relative error of at most 0.02.
Values may be sent and summed in bfloat16 or wider, within the bound.
A program may use at most 64 MiB of HBM per device.

```python
import math
import jax
import jax.numpy as jnp
from jax import lax

D = 1024
HALF_HEADS = 16
HEAD = 64
STATE = 128
KW = 4
D2 = 1536
FF = 4096
BYTES_DEV = 128
DI = 1024
XBC = 1280
PAD = 512
CH_DEV = 32
BYTES = 1024
N_SEQ = 8


def decay_pair(key):
    base_key = jax.random.fold_in(key, 17)
    key_fast, key_rough, random_key_location, random_key_depth, key_step = jax.random.split(base_key, 5)
    overall_row_count = BYTES_DEV * N_SEQ
    fast_heads = jax.random.bernoulli(key_fast, 0.5, (HALF_HEADS,))
    roughness = jnp.exp(jax.random.uniform(key_rough, (overall_row_count, HALF_HEADS), jnp.float32, math.log(0.6), math.log(1.8)))
    rate_increment = jnp.where(fast_heads[None, :], 1.0 / 40.0, 0.3 / overall_row_count) * roughness
    surge_locations = jax.random.randint(random_key_location, (3,), 0, overall_row_count)
    surge_present = jnp.any(lax.iota(jnp.int32, overall_row_count)[:, None] == surge_locations[None, :], axis=1)
    surge_depth = jax.random.uniform(random_key_depth, (overall_row_count, HALF_HEADS), jnp.float32, 0.22, 0.5)
    logarithm_decays = -rate_increment - jnp.where(surge_present[:, None], surge_depth, 0.0)
    factor = jnp.exp(jax.random.uniform(key_step, (overall_row_count, HALF_HEADS), jnp.float32, math.log(0.5), math.log(2.0)))
    steps_drawn = factor * jnp.sqrt(1.0 - jnp.exp(2.0 * logarithm_decays))
    return (logarithm_decays, steps_drawn)


def draw_log_decay(key, part):
    return decay_pair(key)[0]


def draw_step_size(key, part):
    return decay_pair(key)[1]


def shuffle_one(perm_key):
    return jax.random.permutation(perm_key, BYTES_DEV)


def draw_boundaries(key, part):
    base_key = jax.random.fold_in(key, 29)
    key_offsets, key_peak, key_perm = jax.random.split(base_key, 3)
    offsets = jax.random.randint(key_offsets, (N_SEQ,), 0, CH_DEV)
    peak_dev = jax.random.randint(key_peak, (), 0, N_SEQ - 1)
    dev_ids = lax.iota(jnp.int32, N_SEQ)
    offsets = jnp.where(dev_ids == peak_dev, CH_DEV - 1, offsets)
    offsets = jnp.where(dev_ids == peak_dev - 1, 0, offsets)
    offsets = jnp.where(dev_ids == N_SEQ - 1, 0, offsets)
    prior_offsets = jnp.concatenate([jnp.zeros((1,), jnp.int32), offsets[:-1]])
    counts = CH_DEV + offsets - prior_offsets
    perm_keys = jax.random.split(key_perm, N_SEQ)
    orders = jax.vmap(shuffle_one)(perm_keys)
    byte_ranks = jnp.argsort(orders, axis=1).astype(jnp.int32)
    byte_ranks = byte_ranks.at[0, 0].set(-1)
    byte_ranks = jnp.argsort(jnp.argsort(byte_ranks, axis=1), axis=1).astype(jnp.int32)
    chosen_flags = (byte_ranks < counts[:, None]).reshape(N_SEQ * BYTES_DEV)
    return jnp.nonzero(chosen_flags, size=N_SEQ * CH_DEV)[0].astype(jnp.int32)


def level_of(own_key, shape, cuts, low, top_value):
    def one(axis_at, parts):
        heights = jax.random.uniform(jax.random.fold_in(jax.random.fold_in(own_key, 6), axis_at), (parts,), jnp.float32, low / len(cuts), top_value / len(cuts))
        return jnp.repeat(jnp.exp(heights), shape[axis_at] // parts).reshape((-1,) + (1,) * (len(shape) - axis_at - 1))

    factor_of = one(*cuts[0])
    for cut in cuts[1:]:
        factor_of = factor_of * one(*cut)
    return factor_of


def normal_values(rng, dims, spread, limit, pieces=(), held_as=jnp.bfloat16):
    drawn = jax.random.normal(rng, dims, jnp.float32) * spread
    if len(pieces) > 0:
        drawn = level_of(rng, dims, pieces, -0.22, 0.18) * drawn
    return jnp.clip(drawn, min=-limit, max=limit).astype(held_as)


def setup_inputs(seed: int = 0, part: int = 0) -> dict:
    streams_of = jax.random.split(jax.random.key(seed), 15)
    part_keys = jax.random.split(jax.random.fold_in(streams_of[14], part), 15)
    features = normal_values(part_keys[0], (BYTES, XBC), 1.0, 6.0, ((0, 8),))
    gate_in = normal_values(part_keys[1], (BYTES, DI), 1.0, 6.0, ((0, 8),))
    conv_weight = normal_values(streams_of[2], (KW, XBC), 0.5, 3.0, (), jnp.float32)
    conv_bias = jnp.clip(jax.random.uniform(streams_of[3], (XBC,), jnp.float32, -0.5, 0.5), -0.5, 0.5)
    log_decay = draw_log_decay(jax.random.fold_in(jax.random.fold_in(streams_of[14], part), 71), part)
    step_size = draw_step_size(jax.random.fold_in(jax.random.fold_in(streams_of[14], part), 71), part)
    gate_gain = jnp.clip(1.0 + 0.15 * jax.random.normal(streams_of[6], (DI,), jnp.float32), 0.25, 1.75)
    w_out = normal_values(streams_of[7], (DI, D), DI ** -0.5, 0.1875)
    boundaries = draw_boundaries(jax.random.fold_in(jax.random.fold_in(streams_of[14], part), 71), part)
    pad_vector = normal_values(streams_of[9], (PAD,), 1.0, 5.0)
    main_gain = jnp.clip(1.0 + 0.15 * jax.random.normal(streams_of[10], (D2,), jnp.float32), 0.25, 1.75)
    w_gate = normal_values(streams_of[11], (D2, FF), D2 ** -0.5, 0.15625, ((1, 8),))
    w_up = normal_values(streams_of[12], (D2, FF), D2 ** -0.5, 0.15625, ((1, 8),))
    w_down = normal_values(streams_of[13], (FF, D), FF ** -0.5, 0.09375, ((0, 8),))
    return dict(features=features, gate_in=gate_in, conv_weight=conv_weight, conv_bias=conv_bias, log_decay=log_decay, step_size=step_size, gate_gain=gate_gain, w_out=w_out, boundaries=boundaries, pad_vector=pad_vector, main_gain=main_gain, w_gate=w_gate, w_up=w_up, w_down=w_down)


EPSILON = 1e-05

def rms_scale(values):
    return values * lax.rsqrt(lax.optimization_barrier(jnp.mean(values * values, axis=-1, keepdims=True)) + EPSILON)

def reference(features, gate_in, conv_weight, conv_bias, log_decay, step_size, gate_gain, w_out, boundaries, pad_vector, main_gain, w_gate, w_up, w_down):
    overall_row_count = features.shape[0]
    padded = jnp.concatenate([jnp.zeros((KW - 1, XBC), jnp.bfloat16), features], 0)
    conv_mixed = conv_bias[None, :] + jnp.zeros((overall_row_count, XBC), jnp.float32)
    for tap_index in range(KW):
        conv_mixed = conv_mixed + conv_weight[tap_index][None, :] * padded[tap_index:tap_index + overall_row_count].astype(jnp.float32)
    conv_mixed = jax.nn.silu(conv_mixed).astype(jnp.bfloat16)
    x_part = conv_mixed[:, :DI].astype(jnp.float32).reshape(overall_row_count, HALF_HEADS, HEAD)
    b_part = conv_mixed[:, DI:DI + STATE].astype(jnp.float32)
    c_part = conv_mixed[:, DI + STATE:].astype(jnp.float32)

    def advance(ssm_state, step_inputs):
        decay_now, step_now, x_row, b_row, c_row = step_inputs
        ssm_state = jnp.exp(decay_now)[:, None, None] * ssm_state + (step_now[:, None] * x_row)[:, :, None] * b_row[None, None, :]
        read_out = jnp.einsum('hpn,n->hp', ssm_state, c_row, precision=lax.Precision.HIGHEST)
        return (ssm_state, read_out)
    initial = jnp.zeros((HALF_HEADS, HEAD, STATE), jnp.float32)
    _, ssm_out = lax.scan(advance, initial, (log_decay, step_size, x_part, b_part, c_part))
    gated_out = ssm_out.reshape(overall_row_count, DI) * jax.nn.silu(gate_in.astype(jnp.float32))
    normed = (rms_scale(gated_out) * gate_gain).astype(jnp.bfloat16)
    encoded = jnp.dot(normed, w_out, preferred_element_type=jnp.float32).astype(jnp.bfloat16)
    block_rows = jnp.take(encoded, boundaries.astype(jnp.int32), axis=0)
    filler = jnp.broadcast_to(pad_vector[None, :], (block_rows.shape[0], PAD))
    joined = jnp.concatenate([block_rows, filler], 1)
    main_normed = (rms_scale(joined.astype(jnp.float32)) * main_gain).astype(jnp.bfloat16)
    gate_part = jnp.dot(main_normed, w_gate, preferred_element_type=jnp.float32)
    up_part = jnp.dot(main_normed, w_up, preferred_element_type=jnp.float32)
    activated = (jax.nn.silu(gate_part) * up_part).astype(jnp.bfloat16)
    group_width = FF // N_SEQ
    act_groups = activated.reshape(activated.shape[0], N_SEQ, group_width).transpose(1, 0, 2)
    down_groups = w_down.reshape(N_SEQ, group_width, D)

    def add_group(total, group_inputs):
        act_piece, down_piece = group_inputs
        partial_value = jnp.dot(act_piece, down_piece, preferred_element_type=jnp.float32).astype(jnp.bfloat16)
        return (total + partial_value.astype(jnp.float32), None)
    mlp_out, _ = lax.scan(add_group, jnp.zeros((activated.shape[0], D), jnp.float32), (act_groups, down_groups))
    block_out = (block_rows.astype(jnp.float32) + mlp_out).astype(jnp.bfloat16)
    positions = jnp.arange(overall_row_count).astype(jnp.int32)
    block_of = (jnp.searchsorted(boundaries.astype(jnp.int32), positions, side='right') - 1).astype(jnp.int32)
    expanded = jnp.take(block_out, block_of, axis=0)
    return (encoded.astype(jnp.float32) + expanded.astype(jnp.float32)).astype(jnp.bfloat16)
```

```python
import functools

import jax
import jax.numpy as jnp
from jax import lax
from jax.experimental import pallas as pl
from jax.experimental.pallas import tpu as pltpu
from jax.sharding import PartitionSpec as P

EPSILON = 1e-05
TILE = 16
F32 = jnp.float32
BF16 = jnp.bfloat16


def mm(a, b):
    return jnp.dot(a, b, preferred_element_type=F32)


def silu(v):
    return v / (1.0 + jnp.exp(-v))


def kernel(
    n,
    features,
    gate_hbm,
    conv_weight,
    conv_bias,
    log_decay,
    step_size,
    gate_gain,
    w_out_hbm,
    boundaries,
    pad_vector,
    main_gain,
    w_gate_hbm,
    w_up_hbm,
    w_down_hbm,
    out,
    gate_in,
    w_out,
    w_gate,
    w_up,
    w_down,
    halo,
    xs,
    dec,
    sbuf,
    rbuf,
    obuf,
    inbuf,
    enc,
    upper,
    arrived,
    gath,
    nbuf,
    part,
    pair,
    csend,
    crecv,
    table,
    load_sem,
    one_send,
    one_recv,
    dec_send,
    dec_recv,
    st1_send,
    st1_recv,
    st2_send,
    st2_recv,
    ag_send,
    fwd_send,
    ag_recv,
    pair_send,
    pair_recv,
    chip_send,
    chip_recv,
):
    me = lax.axis_index("seq")
    chips = n // 2
    chip, core = lax.div(me, 2), lax.rem(me, 2)
    partner = chip * 2 + (1 - core)
    nxt, prv = lax.rem(me + 1, n), lax.rem(me + n - 1, n)
    rows, channels = features.shape
    heads = log_decay.shape[1]
    inner = gate_in.shape[1]
    head_dim = inner // heads
    state_dim = (channels - inner) // 2
    piece = state_dim // n
    per = gath.shape[1]
    taps = conv_weight.shape[0]

    barrier = pltpu.get_barrier_semaphore()
    for off in range(1, n):
        pl.semaphore_signal(
            barrier,
            inc=1,
            device_id={"seq": lax.rem(me + off, n)},
            device_id_type=pl.DeviceIdType.MESH,
        )

    loads = []
    for i, (src, dst) in enumerate(
        (
            (gate_hbm, gate_in),
            (w_out_hbm, w_out),
            (w_gate_hbm, w_gate),
            (w_up_hbm, w_up),
            (w_down_hbm, w_down),
        )
    ):
        c = pltpu.make_async_copy(src, dst, load_sem.at[i])
        c.start()
        loads.append(c)

    def remote(src, dst, ssem, rsem, peer):
        return pltpu.make_async_remote_copy(
            src_ref=src,
            dst_ref=dst,
            send_sem=ssem,
            recv_sem=rsem,
            device_id={"seq": peer},
            device_id_type=pl.DeviceIdType.MESH,
        )

    row_i = lax.broadcasted_iota(jnp.int32, (rows, rows), 0)
    col_i = lax.broadcasted_iota(jnp.int32, (rows, rows), 1)
    causal = row_i >= col_i
    cum = jnp.dot(
        causal.astype(F32),
        log_decay[...],
        preferred_element_type=F32,
        precision=lax.Precision.HIGHEST,
    )
    total = cum[rows - 1 :, :]
    mid = cum[rows // 2 : rows // 2 + 1, :]
    dec[me] = jnp.zeros(dec.shape[1:], F32)
    dec[me, :, :heads] = jnp.broadcast_to(total, (dec.shape[1], heads))

    pl.semaphore_wait(barrier, n - 1)

    halo_copy = remote(
        features.at[pl.ds(rows - TILE, TILE)], halo, one_send.at[0], one_recv.at[0], nxt
    )
    halo_copy.start()
    dec_copies = []
    for off in range(1, n):
        peer = lax.rem(me + off, n)
        c = remote(dec.at[me], dec.at[me], dec_send.at[peer], dec_recv.at[me], peer)
        c.start()
        dec_copies.append(c)

    hid = lax.broadcasted_iota(jnp.int32, (heads, inner), 0) * head_dim
    lane = lax.broadcasted_iota(jnp.int32, (heads, inner), 1)
    onehot = ((lane >= hid) & (lane < hid + head_dim)).astype(F32).astype(BF16)

    def expand(v):
        hi = v.astype(BF16)
        lo = (v - hi.astype(F32)).astype(BF16)
        return mm(hi, onehot) + mm(lo, onehot)

    in_coef = expand(step_size[...] * jnp.exp(mid - cum))
    out_coef = expand(jnp.exp(cum - mid))
    mid_to_end = expand(jnp.broadcast_to(jnp.exp(total - mid), (8, heads)))[:1]
    start_to_mid = expand(jnp.broadcast_to(jnp.exp(mid), (8, heads)))[:1]

    xs[pl.ds(TILE, rows), :] = features[...].astype(F32)

    bnd = boundaries[...].reshape(1, boundaries.shape[0])
    pos = me * rows + lax.broadcasted_iota(jnp.int32, (rows, 1), 0)
    below = jnp.sum((bnd <= pos).astype(F32), axis=1, keepdims=True).astype(jnp.int32)
    starts = jnp.sum((bnd == pos).astype(F32), axis=1, keepdims=True)
    slot = below - 1 - me * per
    slots = lax.broadcasted_iota(jnp.int32, (rows, 2 * per), 1)
    pick = (jnp.where(slot == slots, 1.0, 0.0) * starts).T.astype(BF16)
    table_rows = table.shape[0]
    entries = lax.broadcasted_iota(jnp.int32, (rows, table_rows), 1)
    spread = jnp.where(slot + TILE == entries, 1.0, 0.0).astype(BF16)

    halo_copy.wait_recv()
    xs[pl.ds(0, TILE), :] = jnp.where(me > 0, halo[...].astype(F32), 0.0)
    mixed = conv_bias[...].reshape(1, channels)
    for k in range(taps):
        mixed = mixed + conv_weight[pl.ds(k, 1), :] * xs[pl.ds(TILE - taps + 1 + k, rows), :]
    mixed = silu(mixed)
    x_in = (mixed[:, :inner].astype(BF16).astype(F32) * in_coef).astype(BF16)
    b32 = mixed[:, inner : inner + state_dim]
    b_part = b32.astype(BF16)
    c_part = mixed[:, inner + state_dim :].astype(BF16)
    state = mm(b32.T.astype(BF16), x_in) * mid_to_end
    for j in range(n):
        sbuf[j] = state[j * piece : (j + 1) * piece].astype(BF16)
    st1 = []
    for off in range(1, n):
        peer = lax.rem(me + off, n)
        c = remote(sbuf.at[peer], rbuf.at[me], st1_send.at[peer], st1_recv.at[me], peer)
        c.start()
        st1.append(c)
    rbuf[me] = sbuf[me]

    prod = lax.dot_general(
        c_part, b_part, (((1,), (1,)), ((), ())), preferred_element_type=F32
    )
    local = mm(jnp.where(causal, prod, 0.0).astype(BF16), x_in)
    loads[0].wait()
    gate = silu(gate_in[...].astype(F32))

    for off in range(1, n):
        src = lax.rem(me + n - off, n)
        remote(dec.at[src], dec.at[src], dec_send.at[src], dec_recv.at[src], src).wait_recv()
    decays = jnp.concatenate([dec[k, 0:1, :] for k in range(n)], axis=0)[:, :heads]
    decays = expand(jnp.exp(decays))
    for off in range(1, n):
        src = lax.rem(me + n - off, n)
        remote(rbuf.at[src], rbuf.at[src], st1_send.at[src], st1_recv.at[src], src).wait_recv()
    before = jnp.zeros((piece, inner), F32)
    for k in range(n):
        obuf[k] = before.astype(BF16)
        before = before * decays[k : k + 1] + rbuf[k].astype(F32)
    st2 = []
    for off in range(1, n):
        peer = lax.rem(me + off, n)
        c = remote(obuf.at[peer], inbuf.at[me], st2_send.at[peer], st2_recv.at[me], peer)
        c.start()
        st2.append(c)
    inbuf[me] = obuf[me]
    for off in range(1, n):
        src = lax.rem(me + n - off, n)
        remote(inbuf.at[src], inbuf.at[src], st2_send.at[src], st2_recv.at[src], src).wait_recv()
    if piece % TILE == 0:
        state_in = inbuf[...].reshape(state_dim, inner)
    else:
        state_in = jnp.concatenate([inbuf[k].astype(F32) for k in range(n)], axis=0).astype(BF16)
    ssm_out = (local + mm(c_part, state_in) * start_to_mid) * out_coef

    gated = ssm_out * gate
    scale = lax.rsqrt(jnp.mean(gated * gated, axis=1, keepdims=True) + EPSILON)
    normed = (gated * scale * gate_gain[...].reshape(1, inner)).astype(BF16)
    loads[1].wait()
    encoded = mm(normed, w_out[...]).astype(BF16)
    enc[...] = encoded
    picked = mm(pick, encoded).astype(BF16)
    upper[...] = picked[per:]
    up_copy = remote(upper, arrived, one_send.at[1], one_recv.at[1], nxt)
    up_copy.start()
    up_copy.wait_recv()
    mine = core * chips + chip
    own_rows = picked[:per].astype(F32) + jnp.where(me > 0, arrived[...].astype(F32), 0.0)
    gath[mine] = own_rows.astype(BF16)

    ag = []
    for off in range(1, chips):
        q = lax.rem(chip + off, chips)
        c = remote(gath.at[mine], gath.at[mine], ag_send.at[q], ag_recv.at[mine], 2 * q + core)
        c.start()
        ag.append(c)
    c = remote(gath.at[mine], gath.at[mine], fwd_send.at[chip], ag_recv.at[mine], partner)
    c.start()
    ag.append(c)
    for off in range(1, chips):
        s = core * chips + lax.rem(chip + chips - off, chips)
        q = lax.rem(chip + chips - off, chips)
        remote(gath.at[s], gath.at[s], ag_send.at[q], ag_recv.at[s], 2 * q + core).wait_recv()
        c = remote(gath.at[s], gath.at[s], fwd_send.at[q], ag_recv.at[s], partner)
        c.start()
        ag.append(c)

    main_width = main_gain.shape[0]
    width = out.shape[1]
    half = chips * per
    gain = main_gain[...].reshape(1, main_width)
    pad = pad_vector[...].astype(F32).reshape(1, main_width - width)
    pad_sum = jnp.sum(pad * pad, axis=1, keepdims=True)
    pad_gain = pad * gain[:, width:]

    def hidden(which):
        rows_in = gath[pl.ds(which * chips, chips)].reshape(half, width).astype(F32)
        mean = (jnp.sum(rows_in * rows_in, axis=1, keepdims=True) + pad_sum) / main_width
        scale = lax.rsqrt(mean + EPSILON)
        nbuf[:, :width] = (rows_in * scale * gain[:, :width]).astype(BF16)
        nbuf[:, width:] = (scale * pad_gain).astype(BF16)
        act = nbuf[...]
        return (silu(mm(act, w_gate[...])) * mm(act, w_up[...])).astype(BF16)

    loads[2].wait()
    loads[3].wait()
    act_own = hidden(core)
    for q in range(chips):
        s = (1 - core) * chips + q
        remote(gath.at[s], gath.at[s], fwd_send.at[q], ag_recv.at[s], partner).wait_recv()
    act_other = hidden(1 - core)
    loads[4].wait()
    part[...] = mm(act_other, w_down[...]).astype(BF16).reshape(chips, per, width)
    rs = []
    for q in range(chips):
        c = remote(part.at[q], pair.at[q], pair_send.at[q], pair_recv.at[q], partner)
        c.start()
        rs.append(c)
    own_part = mm(act_own, w_down[...]).reshape(chips, per, width)
    for q in range(chips):
        remote(part.at[q], pair.at[q], pair_send.at[q], pair_recv.at[q], partner).wait_recv()
    csend[...] = (own_part + pair[...].astype(F32)).astype(BF16)
    for off in range(1, chips):
        q = lax.rem(chip + off, chips)
        c = remote(csend.at[q], crecv.at[chip], chip_send.at[q], chip_recv.at[chip], 2 * q + core)
        c.start()
        rs.append(c)
    result = own_rows + csend[chip].astype(F32)
    for off in range(1, chips):
        q = lax.rem(chip + chips - off, chips)
        remote(csend.at[q], crecv.at[q], chip_send.at[q], chip_recv.at[q], 2 * q + core).wait_recv()
        result = result + crecv[q].astype(F32)
    table[pl.ds(TILE, per), :] = result.astype(BF16)
    fol = remote(
        table.at[pl.ds(TILE, per)],
        table.at[pl.ds(TILE + per, per)],
        one_send.at[2],
        one_recv.at[2],
        prv,
    )
    fol.start()
    ear = remote(
        table.at[pl.ds(per, TILE)],
        table.at[pl.ds(0, TILE)],
        one_send.at[3],
        one_recv.at[3],
        nxt,
    )
    ear.start()
    fol.wait_recv()
    ear.wait_recv()
    expanded = mm(spread, table[...])
    out[...] = (enc[...].astype(F32) + expanded).astype(BF16)

    for c in [halo_copy, up_copy, fol, ear] + dec_copies + st1 + st2 + ag + rs:
        c.wait_send()


def per_device(
    n,
    features,
    gate_in,
    conv_weight,
    conv_bias,
    log_decay,
    step_size,
    gate_gain,
    w_out,
    boundaries,
    pad_vector,
    main_gain,
    w_gate,
    w_up,
    w_down,
):
    rows, channels = features.shape
    inner = gate_in.shape[1]
    width = w_out.shape[1]
    state_dim = (channels - inner) // 2
    piece = state_dim // n
    chips = n // 2
    per = boundaries.shape[0] // n
    half = chips * per
    vmem = pl.BlockSpec(memory_space=pltpu.VMEM)
    hbm = pl.BlockSpec(memory_space=pl.ANY)
    dma = pltpu.SemaphoreType.DMA
    in_hbm = (1, 7, 11, 12, 13)
    return pl.pallas_call(
        functools.partial(kernel, n),
        out_shape=jax.ShapeDtypeStruct((rows, width), BF16),
        in_specs=[hbm if i in in_hbm else vmem for i in range(14)],
        out_specs=vmem,
        scratch_shapes=[
            pltpu.VMEM(gate_in.shape, BF16),
            pltpu.VMEM(w_out.shape, BF16),
            pltpu.VMEM(w_gate.shape, BF16),
            pltpu.VMEM(w_up.shape, BF16),
            pltpu.VMEM(w_down.shape, BF16),
            pltpu.VMEM((TILE, channels), BF16),
            pltpu.VMEM((TILE + rows, channels), F32),
            pltpu.VMEM((n, 8, 128), F32),
            pltpu.VMEM((n, piece, inner), BF16),
            pltpu.VMEM((n, piece, inner), BF16),
            pltpu.VMEM((n, piece, inner), BF16),
            pltpu.VMEM((n, piece, inner), BF16),
            pltpu.VMEM((rows, width), BF16),
            pltpu.VMEM((per, width), BF16),
            pltpu.VMEM((per, width), BF16),
            pltpu.VMEM((n, per, width), BF16),
            pltpu.VMEM((half, main_gain.shape[0]), BF16),
            pltpu.VMEM((chips, per, width), BF16),
            pltpu.VMEM((chips, per, width), BF16),
            pltpu.VMEM((chips, per, width), BF16),
            pltpu.VMEM((chips, per, width), BF16),
            pltpu.VMEM((TILE + 2 * per, width), BF16),
            dma((5,)),
            dma((4,)),
            dma((4,)),
            dma((n,)),
            dma((n,)),
            dma((n,)),
            dma((n,)),
            dma((n,)),
            dma((n,)),
            dma((chips,)),
            dma((chips,)),
            dma((n,)),
            dma((chips,)),
            dma((chips,)),
            dma((chips,)),
            dma((chips,)),
        ],
        compiler_params=pltpu.CompilerParams(collective_id=0, has_side_effects=True),
    )(
        features,
        gate_in,
        conv_weight,
        conv_bias,
        log_decay,
        step_size,
        gate_gain,
        w_out,
        boundaries,
        pad_vector,
        main_gain,
        w_gate,
        w_up,
        w_down,
    )


def solution(mesh):
    in_specs = (
        P(("doc", "seq"), None),
        P(("doc", "seq"), None),
        P(),
        P(),
        P(("doc", "seq"), None),
        P(("doc", "seq"), None),
        P(),
        P(),
        P("doc"),
        P(),
        P(),
        P(None, "seq"),
        P(None, "seq"),
        P("seq", None),
    )
    out_specs = P(("doc", "seq"), None)
    return jax.shard_map(
        functools.partial(per_device, mesh.shape["seq"]),
        mesh=mesh,
        in_specs=in_specs,
        out_specs=out_specs,
        check_vma=False,
    )
```

```python
import functools

import jax
import jax.numpy as jnp
from jax import lax
from jax.experimental import pallas as pl
from jax.experimental.pallas import tpu as pltpu
from jax.sharding import PartitionSpec as P

EPSILON = 1e-05
TILE = 16
F32 = jnp.float32
BF16 = jnp.bfloat16


def mm(a, b):
    return jnp.dot(a, b, preferred_element_type=F32)


def silu(v):
    return v / (1.0 + jnp.exp(-v))


def kernel(
    n,
    per,
    features_hbm,
    gate_in_hbm,
    conv_weight_hbm,
    conv_bias_hbm,
    log_decay_hbm,
    step_size_hbm,
    gate_gain_hbm,
    w_out_hbm,
    boundaries_hbm,
    pad_vector_hbm,
    main_gain_hbm,
    w_gate_hbm,
    w_up_hbm,
    w_down_hbm,
    out,
    features,
    gate_in,
    conv_weight,
    conv_bias,
    log_decay,
    step_size,
    gate_gain,
    w_out,
    boundaries,
    pad_vector,
    main_gain,
    w_gate,
    w_up,
    w_down,
    halo,
    xs,
    dec,
    sbuf,
    rbuf,
    obuf,
    inbuf,
    enc,
    upper,
    arrived,
    gath,
    nbuf,
    part,
    pair,
    csend,
    crecv,
    own_part,
    x_buf,
    bc_buf,
    table,
    load_sem,
    one_send,
    one_recv,
    dec_send,
    dec_recv,
    st1_send,
    st1_recv,
    st2_send,
    st2_recv,
    ag_send,
    fwd_send,
    ag_recv,
    pair_send,
    pair_recv,
    chip_send,
    chip_recv,
):
    me = lax.axis_index("seq")
    chips = n // 2
    chip, core = lax.div(me, 2), lax.rem(me, 2)
    partner = chip * 2 + (1 - core)
    nxt, prv = lax.rem(me + 1, n), lax.rem(me + n - 1, n)
    rows, channels = features.shape
    heads = log_decay.shape[0]
    inner = gate_in.shape[1]
    head_dim = inner // heads
    state_dim = (channels - inner) // 2
    piece = state_dim // n
    taps = conv_weight.shape[0]

    barrier = pltpu.get_barrier_semaphore()
    for off in range(1, n):
        pl.semaphore_signal(
            barrier,
            inc=1,
            device_id={"seq": lax.rem(me + off, n)},
            device_id_type=pl.DeviceIdType.MESH,
        )

    order = (
        (log_decay_hbm, log_decay),
        (features_hbm, features),
        (step_size_hbm, step_size),
        (conv_weight_hbm, conv_weight),
        (conv_bias_hbm, conv_bias),
        (boundaries_hbm, boundaries),
        (gate_in_hbm, gate_in),
        (gate_gain_hbm, gate_gain),
        (w_out_hbm, w_out),
        (pad_vector_hbm, pad_vector),
        (main_gain_hbm, main_gain),
        (w_gate_hbm, w_gate),
        (w_up_hbm, w_up),
        (w_down_hbm, w_down),
    )
    loads = []
    for i, (src, dst) in enumerate(order):
        c = pltpu.make_async_copy(src, dst, load_sem.at[i])
        c.start()
        loads.append(c)

    def remote(src, dst, ssem, rsem, peer):
        return pltpu.make_async_remote_copy(
            src_ref=src,
            dst_ref=dst,
            send_sem=ssem,
            recv_sem=rsem,
            device_id={"seq": peer},
            device_id_type=pl.DeviceIdType.MESH,
        )

    row_i = lax.broadcasted_iota(jnp.int32, (rows, rows), 0)
    col_i = lax.broadcasted_iota(jnp.int32, (rows, rows), 1)
    causal = row_i >= col_i
    loads[0].wait()
    cum = jnp.dot(
        causal.astype(F32),
        log_decay[...].T,
        preferred_element_type=F32,
        precision=lax.Precision.HIGHEST,
    )
    total = cum[rows - 1 :, :]
    mid = cum[rows // 2 : rows // 2 + 1, :]
    dec[me] = jnp.zeros(dec.shape[1:], F32)
    dec[me, :, :heads] = jnp.broadcast_to(total, (dec.shape[1], heads))

    for c in loads[1:6]:
        c.wait()
    pl.semaphore_wait(barrier, n - 1)

    halo_copy = remote(
        features.at[pl.ds(rows - TILE, TILE)], halo, one_send.at[0], one_recv.at[0], nxt
    )
    halo_copy.start()
    dec_copies = []
    for off in range(1, n):
        peer = lax.rem(me + off, n)
        c = remote(dec.at[me], dec.at[me], dec_send.at[peer], dec_recv.at[me], peer)
        c.start()
        dec_copies.append(c)

    hid = lax.broadcasted_iota(jnp.int32, (heads, inner), 0) * head_dim
    lane = lax.broadcasted_iota(jnp.int32, (heads, inner), 1)
    onehot = ((lane >= hid) & (lane < hid + head_dim)).astype(F32).astype(BF16)

    def expand(v):
        hi = v.astype(BF16)
        lo = (v - hi.astype(F32)).astype(BF16)
        return mm(hi, onehot) + mm(lo, onehot)

    in_coef = expand(step_size[...].T * jnp.exp(mid - cum))
    out_coef = expand(jnp.exp(cum - mid))
    mid_to_end = expand(jnp.broadcast_to(jnp.exp(total - mid), (8, heads)))[:1]
    start_to_mid = expand(jnp.broadcast_to(jnp.exp(mid), (8, heads)))[:1]

    xs[pl.ds(TILE, rows), :] = features[...].astype(F32)

    def convolved(first, count):
        mixed = conv_bias[...].reshape(1, channels)
        for k in range(taps):
            mixed = mixed + conv_weight[pl.ds(k, 1), :] * xs[
                pl.ds(TILE - taps + 1 + first + k, count), :
            ]
        mixed = silu(mixed)
        coef = in_coef[first : first + count]
        x_new = (mixed[:, :inner].astype(BF16).astype(F32) * coef).astype(BF16)
        x_buf[pl.ds(first, count), :] = x_new
        bc_buf[pl.ds(first, count), :] = mixed[:, inner:].astype(BF16)
        b_new = mixed[:, inner : inner + state_dim]
        return mm(b_new.T.astype(BF16), x_new)

    state = convolved(TILE, rows - TILE)

    bnd = boundaries[...].reshape(1, boundaries.shape[0])
    pos = me * rows + lax.broadcasted_iota(jnp.int32, (rows, 1), 0)
    below = jnp.sum((bnd <= pos).astype(F32), axis=1, keepdims=True).astype(jnp.int32)
    starts = jnp.sum((bnd == pos).astype(F32), axis=1, keepdims=True)
    slot = below - 1 - me * per
    slots = lax.broadcasted_iota(jnp.int32, (rows, 2 * per), 1)
    pick = (jnp.where(slot == slots, 1.0, 0.0) * starts).T.astype(BF16)
    table_rows = table.shape[0]
    entries = lax.broadcasted_iota(jnp.int32, (rows, table_rows), 1)
    spread = jnp.where(slot + TILE == entries, 1.0, 0.0).astype(BF16)

    halo_copy.wait_recv()
    xs[pl.ds(0, TILE), :] = jnp.where(me > 0, halo[...].astype(F32), 0.0)
    state = (state + convolved(0, TILE)) * mid_to_end
    for j in range(n):
        sbuf[j] = state[j * piece : (j + 1) * piece].astype(BF16)
    st1 = []
    for off in range(1, n):
        peer = lax.rem(me + off, n)
        c = remote(sbuf.at[peer], rbuf.at[me], st1_send.at[peer], st1_recv.at[me], peer)
        c.start()
        st1.append(c)
    rbuf[me] = sbuf[me]

    x_in = x_buf[...]
    b_part = bc_buf[:, :state_dim]
    c_part = bc_buf[:, state_dim:]
    prod = lax.dot_general(
        c_part, b_part, (((1,), (1,)), ((), ())), preferred_element_type=F32
    )
    local = mm(jnp.where(causal, prod, 0.0).astype(BF16), x_in)
    loads[6].wait()
    loads[7].wait()
    gate = silu(gate_in[...].astype(F32))

    for off in range(1, n):
        src = lax.rem(me + n - off, n)
        remote(dec.at[src], dec.at[src], dec_send.at[src], dec_recv.at[src], src).wait_recv()
    decays = jnp.concatenate([dec[k, 0:1, :] for k in range(n)], axis=0)[:, :heads]
    decays = expand(jnp.exp(decays))
    for off in range(1, n):
        src = lax.rem(me + n - off, n)
        remote(rbuf.at[src], rbuf.at[src], st1_send.at[src], st1_recv.at[src], src).wait_recv()
    before = jnp.zeros((piece, inner), F32)
    for k in range(n):
        obuf[k] = before.astype(BF16)
        before = before * decays[k : k + 1] + rbuf[k].astype(F32)
    st2 = []
    for off in range(1, n):
        peer = lax.rem(me + off, n)
        c = remote(obuf.at[peer], inbuf.at[me], st2_send.at[peer], st2_recv.at[me], peer)
        c.start()
        st2.append(c)
    inbuf[me] = obuf[me]
    for off in range(1, n):
        src = lax.rem(me + n - off, n)
        remote(inbuf.at[src], inbuf.at[src], st2_send.at[src], st2_recv.at[src], src).wait_recv()
    if piece % TILE == 0:
        state_in = inbuf[...].reshape(state_dim, inner)
    else:
        state_in = jnp.concatenate([inbuf[k].astype(F32) for k in range(n)], axis=0).astype(BF16)
    ssm_out = (local + mm(c_part, state_in) * start_to_mid) * out_coef

    gated = ssm_out * gate
    scale = lax.rsqrt(jnp.mean(gated * gated, axis=1, keepdims=True) + EPSILON)
    normed = (gated * scale * gate_gain[...].reshape(1, inner)).astype(BF16)
    loads[8].wait()
    encoded = mm(normed, w_out[...]).astype(BF16)
    enc[...] = encoded
    picked = mm(pick, encoded).astype(BF16)
    upper[...] = picked[per:]
    up_copy = remote(upper, arrived, one_send.at[1], one_recv.at[1], nxt)
    up_copy.start()
    up_copy.wait_recv()
    mine = core * chips + chip
    own_rows = picked[:per].astype(F32) + jnp.where(me > 0, arrived[...].astype(F32), 0.0)
    gath[mine] = own_rows.astype(BF16)

    ag = []
    for off in range(1, chips):
        q = lax.rem(chip + off, chips)
        c = remote(gath.at[mine], gath.at[mine], ag_send.at[q], ag_recv.at[mine], 2 * q + core)
        c.start()
        ag.append(c)
    c = remote(gath.at[mine], gath.at[mine], fwd_send.at[chip], ag_recv.at[mine], partner)
    c.start()
    ag.append(c)
    for off in range(1, chips):
        s = core * chips + lax.rem(chip + chips - off, chips)
        q = lax.rem(chip + chips - off, chips)
        remote(gath.at[s], gath.at[s], ag_send.at[q], ag_recv.at[s], 2 * q + core).wait_recv()
        c = remote(gath.at[s], gath.at[s], fwd_send.at[q], ag_recv.at[s], partner)
        c.start()
        ag.append(c)

    loads[9].wait()
    loads[10].wait()
    main_width = main_gain.shape[0]
    width = out.shape[1]
    half = chips * per
    gain = main_gain[...].reshape(1, main_width)
    pad = pad_vector[...].astype(F32).reshape(1, main_width - width)
    pad_sum = jnp.sum(pad * pad, axis=1, keepdims=True)
    pad_gain = pad * gain[:, width:]

    def hidden(which):
        rows_in = gath[pl.ds(which * chips, chips)].reshape(half, width).astype(F32)
        mean = (jnp.sum(rows_in * rows_in, axis=1, keepdims=True) + pad_sum) / main_width
        scale = lax.rsqrt(mean + EPSILON)
        nbuf[:, :width] = (rows_in * scale * gain[:, :width]).astype(BF16)
        nbuf[:, width:] = (scale * pad_gain).astype(BF16)
        act = nbuf[...]
        return (silu(mm(act, w_gate[...])) * mm(act, w_up[...])).astype(BF16)

    loads[11].wait()
    loads[12].wait()
    act_own = hidden(core)
    for q in range(chips):
        s = (1 - core) * chips + q
        remote(gath.at[s], gath.at[s], fwd_send.at[q], ag_recv.at[s], partner).wait_recv()
    act_other = hidden(1 - core)
    loads[13].wait()
    part[...] = mm(act_other, w_down[...]).astype(BF16).reshape(chips, per, width)
    rs = []
    targets = [lax.rem(chip + off, chips) for off in range(1, chips)] + [chip]
    for q in targets:
        c = remote(part.at[q], pair.at[q], pair_send.at[q], pair_recv.at[q], partner)
        c.start()
        rs.append(c)
    own_part[...] = mm(act_own, w_down[...]).reshape(chips, per, width)
    for i, q in enumerate(targets):
        remote(part.at[q], pair.at[q], pair_send.at[q], pair_recv.at[q], partner).wait_recv()
        csend[q] = (own_part[q] + pair[q].astype(F32)).astype(BF16)
        if i < chips - 1:
            c = remote(
                csend.at[q], crecv.at[chip], chip_send.at[q], chip_recv.at[chip], 2 * q + core
            )
            c.start()
            rs.append(c)
    result = own_rows + csend[chip].astype(F32)
    for off in range(1, chips):
        q = lax.rem(chip + chips - off, chips)
        remote(csend.at[q], crecv.at[q], chip_send.at[q], chip_recv.at[q], 2 * q + core).wait_recv()
        result = result + crecv[q].astype(F32)
    table[pl.ds(TILE, per), :] = result.astype(BF16)
    fol = remote(
        table.at[pl.ds(TILE, per)],
        table.at[pl.ds(TILE + per, per)],
        one_send.at[2],
        one_recv.at[2],
        prv,
    )
    fol.start()
    ear = remote(
        table.at[pl.ds(per, TILE)],
        table.at[pl.ds(0, TILE)],
        one_send.at[3],
        one_recv.at[3],
        nxt,
    )
    ear.start()
    fol.wait_recv()
    ear.wait_recv()
    expanded = mm(spread, table[...])
    out[...] = (enc[...].astype(F32) + expanded).astype(BF16)

    for c in [halo_copy, up_copy, fol, ear] + dec_copies + st1 + st2 + ag + rs:
        c.wait_send()


def per_device(
    n,
    features,
    gate_in,
    conv_weight,
    conv_bias,
    log_decay,
    step_size,
    gate_gain,
    w_out,
    boundaries,
    pad_vector,
    main_gain,
    w_gate,
    w_up,
    w_down,
):
    rows, channels = features.shape
    inner = gate_in.shape[1]
    width = w_out.shape[1]
    state_dim = (channels - inner) // 2
    piece = state_dim // n
    chips = n // 2
    per = boundaries.shape[0] // n
    half = chips * per
    vmem = pl.BlockSpec(memory_space=pltpu.VMEM)
    hbm = pl.BlockSpec(memory_space=pl.ANY)
    dma = pltpu.SemaphoreType.DMA
    args = (
        features,
        gate_in,
        conv_weight,
        conv_bias,
        log_decay.T,
        step_size.T,
        gate_gain,
        w_out,
        boundaries,
        pad_vector,
        main_gain,
        w_gate,
        w_up,
        w_down,
    )
    return pl.pallas_call(
        functools.partial(kernel, n, per),
        out_shape=jax.ShapeDtypeStruct((rows, width), BF16),
        in_specs=[hbm] * len(args),
        out_specs=vmem,
        scratch_shapes=[
            *[pltpu.VMEM(a.shape, a.dtype) for a in args],
            pltpu.VMEM((TILE, channels), BF16),
            pltpu.VMEM((TILE + rows, channels), F32),
            pltpu.VMEM((n, 8, 128), F32),
            pltpu.VMEM((n, piece, inner), BF16),
            pltpu.VMEM((n, piece, inner), BF16),
            pltpu.VMEM((n, piece, inner), BF16),
            pltpu.VMEM((n, piece, inner), BF16),
            pltpu.VMEM((rows, width), BF16),
            pltpu.VMEM((per, width), BF16),
            pltpu.VMEM((per, width), BF16),
            pltpu.VMEM((n, per, width), BF16),
            pltpu.VMEM((half, main_gain.shape[0]), BF16),
            pltpu.VMEM((chips, per, width), BF16),
            pltpu.VMEM((chips, per, width), BF16),
            pltpu.VMEM((chips, per, width), BF16),
            pltpu.VMEM((chips, per, width), BF16),
            pltpu.VMEM((chips, per, width), F32),
            pltpu.VMEM((rows, inner), BF16),
            pltpu.VMEM((rows, 2 * state_dim), BF16),
            pltpu.VMEM((TILE + 2 * per, width), BF16),
            dma((len(args),)),
            dma((4,)),
            dma((4,)),
            dma((n,)),
            dma((n,)),
            dma((n,)),
            dma((n,)),
            dma((n,)),
            dma((n,)),
            dma((chips,)),
            dma((chips,)),
            dma((n,)),
            dma((chips,)),
            dma((chips,)),
            dma((chips,)),
            dma((chips,)),
        ],
        compiler_params=pltpu.CompilerParams(collective_id=0, has_side_effects=True),
    )(*args)


def solution(mesh):
    in_specs = (
        P(("doc", "seq"), None),
        P(("doc", "seq"), None),
        P(),
        P(),
        P(("doc", "seq"), None),
        P(("doc", "seq"), None),
        P(),
        P(),
        P("doc"),
        P(),
        P(),
        P(None, "seq"),
        P(None, "seq"),
        P("seq", None),
    )
    out_specs = P(("doc", "seq"), None)
    return jax.shard_map(
        functools.partial(per_device, mesh.shape["seq"]),
        mesh=mesh,
        in_specs=in_specs,
        out_specs=out_specs,
        check_vma=False,
    )
```

```python
import functools

import jax
import jax.numpy as jnp
from jax import lax
from jax.experimental import pallas as pl
from jax.experimental.pallas import tpu as pltpu
from jax.sharding import PartitionSpec as P

EPSILON = 1e-05
TILE = 16
F32 = jnp.float32
BF16 = jnp.bfloat16


def mm(a, b):
    return jnp.dot(a, b, preferred_element_type=F32)


def silu(v):
    return v / (1.0 + jnp.exp(-v))


def kernel(
    n,
    per,
    features_hbm,
    gate_in_hbm,
    conv_weight_hbm,
    conv_bias_hbm,
    log_decay_hbm,
    step_size_hbm,
    gate_gain_hbm,
    w_out_hbm,
    boundaries_hbm,
    pad_vector_hbm,
    main_gain_hbm,
    w_gate_hbm,
    w_up_hbm,
    w_down_hbm,
    out,
    features,
    gate_in,
    conv_weight,
    conv_bias,
    log_decay,
    step_size,
    gate_gain,
    w_out,
    boundaries,
    pad_vector,
    main_gain,
    w_gate,
    w_up,
    w_down,
    halo,
    xs,
    dec,
    sbuf,
    rbuf,
    obuf,
    inbuf,
    enc,
    upper,
    arrived,
    gath,
    nbuf,
    part,
    pair,
    csend,
    crecv,
    own_part,
    ubuf,
    hbuf,
    x_buf,
    bc_buf,
    table,
    load_sem,
    one_send,
    one_recv,
    dec_send,
    dec_recv,
    st1_send,
    st1_recv,
    st2_send,
    st2_recv,
    ag_send,
    fwd_send,
    ag_recv,
    pair_send,
    pair_recv,
    chip_send,
    chip_recv,
    u_send,
    uf_send,
    u_recv,
):
    me = lax.axis_index("seq")
    chips = n // 2
    chip, core = lax.div(me, 2), lax.rem(me, 2)
    partner = chip * 2 + (1 - core)
    nxt, prv = lax.rem(me + 1, n), lax.rem(me + n - 1, n)
    rows, channels = features.shape
    heads = log_decay.shape[0]
    inner = gate_in.shape[1]
    head_dim = inner // heads
    state_dim = (channels - inner) // 2
    piece = state_dim // n
    taps = conv_weight.shape[0]

    arrived[...] = jnp.zeros(arrived.shape, BF16)
    barrier = pltpu.get_barrier_semaphore()
    for off in range(1, n):
        pl.semaphore_signal(
            barrier,
            inc=1,
            device_id={"seq": lax.rem(me + off, n)},
            device_id_type=pl.DeviceIdType.MESH,
        )

    order = (
        (log_decay_hbm, log_decay),
        (features_hbm, features),
        (step_size_hbm, step_size),
        (conv_weight_hbm, conv_weight),
        (conv_bias_hbm, conv_bias),
        (boundaries_hbm, boundaries),
        (gate_in_hbm, gate_in),
        (gate_gain_hbm, gate_gain),
        (w_out_hbm, w_out),
        (pad_vector_hbm, pad_vector),
        (main_gain_hbm, main_gain),
        (w_gate_hbm, w_gate),
        (w_up_hbm, w_up),
        (w_down_hbm, w_down),
    )
    loads = []
    for i, (src, dst) in enumerate(order):
        c = pltpu.make_async_copy(src, dst, load_sem.at[i])
        c.start()
        loads.append(c)

    def remote(src, dst, ssem, rsem, peer):
        return pltpu.make_async_remote_copy(
            src_ref=src,
            dst_ref=dst,
            send_sem=ssem,
            recv_sem=rsem,
            device_id={"seq": peer},
            device_id_type=pl.DeviceIdType.MESH,
        )

    row_i = lax.broadcasted_iota(jnp.int32, (rows, rows), 0)
    col_i = lax.broadcasted_iota(jnp.int32, (rows, rows), 1)
    causal = row_i >= col_i
    loads[0].wait()
    cum = jnp.dot(
        causal.astype(F32),
        log_decay[...].T,
        preferred_element_type=F32,
        precision=lax.Precision.HIGHEST,
    )
    total = cum[rows - 1 :, :]
    mid = cum[rows // 2 : rows // 2 + 1, :]
    dec[me] = jnp.zeros(dec.shape[1:], F32)
    dec[me, :, :heads] = jnp.broadcast_to(total, (dec.shape[1], heads))

    for c in loads[1:6]:
        c.wait()
    pl.semaphore_wait(barrier, n - 1)

    halo_copy = remote(
        features.at[pl.ds(rows - TILE, TILE)], halo, one_send.at[0], one_recv.at[0], nxt
    )
    halo_copy.start()
    dec_copies = []
    for off in range(1, n):
        peer = lax.rem(me + off, n)
        c = remote(dec.at[me], dec.at[me], dec_send.at[peer], dec_recv.at[me], peer)
        c.start()
        dec_copies.append(c)

    hid = lax.broadcasted_iota(jnp.int32, (heads, inner), 0) * head_dim
    lane = lax.broadcasted_iota(jnp.int32, (heads, inner), 1)
    onehot = ((lane >= hid) & (lane < hid + head_dim)).astype(F32).astype(BF16)

    def expand(v):
        hi = v.astype(BF16)
        lo = (v - hi.astype(F32)).astype(BF16)
        return mm(hi, onehot) + mm(lo, onehot)

    in_coef = expand(step_size[...].T * jnp.exp(mid - cum))
    out_coef = expand(jnp.exp(cum - mid))
    mid_to_end = expand(jnp.broadcast_to(jnp.exp(total - mid), (8, heads)))[:1]
    start_to_mid = expand(jnp.broadcast_to(jnp.exp(mid), (8, heads)))[:1]

    xs[pl.ds(TILE, rows), :] = features[...].astype(F32)

    def convolved(first, count):
        mixed = conv_bias[...].reshape(1, channels)
        for k in range(taps):
            mixed = mixed + conv_weight[pl.ds(k, 1), :] * xs[
                pl.ds(TILE - taps + 1 + first + k, count), :
            ]
        mixed = silu(mixed)
        coef = in_coef[first : first + count]
        x_new = (mixed[:, :inner].astype(BF16).astype(F32) * coef).astype(BF16)
        x_buf[pl.ds(first, count), :] = x_new
        bc_buf[pl.ds(first, count), :] = mixed[:, inner:].astype(BF16)
        b_new = mixed[:, inner : inner + state_dim]
        return mm(b_new.T.astype(BF16), x_new)

    state = convolved(TILE, rows - TILE)

    bnd = boundaries[...].reshape(1, boundaries.shape[0])
    pos = me * rows + lax.broadcasted_iota(jnp.int32, (rows, 1), 0)
    below = jnp.sum((bnd <= pos).astype(F32), axis=1, keepdims=True).astype(jnp.int32)
    starts = jnp.sum((bnd == pos).astype(F32), axis=1, keepdims=True)
    slot = below - 1 - me * per
    slots = lax.broadcasted_iota(jnp.int32, (rows, 2 * per), 1)
    pick = (jnp.where(slot == slots, 1.0, 0.0) * starts).T.astype(BF16)
    table_rows = table.shape[0]
    entries = lax.broadcasted_iota(jnp.int32, (rows, table_rows), 1)
    spread = jnp.where(slot + TILE == entries, 1.0, 0.0).astype(BF16)

    halo_copy.wait_recv()
    xs[pl.ds(0, TILE), :] = jnp.where(me > 0, halo[...].astype(F32), 0.0)
    state = (state + convolved(0, TILE)) * mid_to_end
    for j in range(n):
        sbuf[j] = state[j * piece : (j + 1) * piece].astype(BF16)
    st1 = []
    for off in range(1, n):
        peer = lax.rem(me + off, n)
        c = remote(sbuf.at[peer], rbuf.at[me], st1_send.at[peer], st1_recv.at[me], peer)
        c.start()
        st1.append(c)
    rbuf[me] = sbuf[me]

    x_in = x_buf[...]
    b_part = bc_buf[:, :state_dim]
    c_part = bc_buf[:, state_dim:]
    prod = lax.dot_general(
        c_part, b_part, (((1,), (1,)), ((), ())), preferred_element_type=F32
    )
    local = mm(jnp.where(causal, prod, 0.0).astype(BF16), x_in)
    loads[6].wait()
    loads[7].wait()
    gate = silu(gate_in[...].astype(F32))

    for off in range(1, n):
        src = lax.rem(me + n - off, n)
        remote(dec.at[src], dec.at[src], dec_send.at[src], dec_recv.at[src], src).wait_recv()
    decays = jnp.concatenate([dec[k, 0:1, :] for k in range(n)], axis=0)[:, :heads]
    decays = expand(jnp.exp(decays))
    for off in range(1, n):
        src = lax.rem(me + n - off, n)
        remote(rbuf.at[src], rbuf.at[src], st1_send.at[src], st1_recv.at[src], src).wait_recv()
    before = jnp.zeros((piece, inner), F32)
    for k in range(n):
        obuf[k] = before.astype(BF16)
        before = before * decays[k : k + 1] + rbuf[k].astype(F32)
    st2 = []
    for off in range(1, n):
        peer = lax.rem(me + off, n)
        c = remote(obuf.at[peer], inbuf.at[me], st2_send.at[peer], st2_recv.at[me], peer)
        c.start()
        st2.append(c)
    inbuf[me] = obuf[me]
    for off in range(1, n):
        src = lax.rem(me + n - off, n)
        remote(inbuf.at[src], inbuf.at[src], st2_send.at[src], st2_recv.at[src], src).wait_recv()
    if piece % TILE == 0:
        state_in = inbuf[...].reshape(state_dim, inner)
    else:
        state_in = jnp.concatenate([inbuf[k].astype(F32) for k in range(n)], axis=0).astype(BF16)
    ssm_out = (local + mm(c_part, state_in) * start_to_mid) * out_coef

    gated = ssm_out * gate
    scale = lax.rsqrt(jnp.mean(gated * gated, axis=1, keepdims=True) + EPSILON)
    normed = (gated * scale * gate_gain[...].reshape(1, inner)).astype(BF16)
    loads[8].wait()
    encoded = mm(normed, w_out[...]).astype(BF16)
    enc[...] = encoded
    picked = mm(pick, encoded).astype(BF16)
    upper[...] = picked[per:]
    mine = core * chips + chip
    others = [lax.rem(chip + off, chips) for off in range(1, chips)]
    sources = [lax.rem(chip + chips - off, chips) for off in range(1, chips)]

    up_copy = remote(upper, arrived, one_send.at[1], one_recv.at[1], partner)
    u_copies = [
        remote(upper, ubuf.at[chip], u_send.at[q], u_recv.at[chip], 2 * q + core) for q in others
    ]
    u_copies.append(remote(upper, ubuf.at[chip], uf_send.at[chip], u_recv.at[chip], partner))

    @pl.when(core == 0)
    def _():
        up_copy.start()

    @pl.when(core == 1)
    def _():
        for c in u_copies:
            c.start()
        ubuf[chip] = upper[...]
        up_copy.wait_recv()

    gath[mine] = (
        picked[:per].astype(F32) + jnp.where(core == 1, arrived[...].astype(F32), 0.0)
    ).astype(BF16)

    ag = []
    for q in others:
        c = remote(gath.at[mine], gath.at[mine], ag_send.at[q], ag_recv.at[mine], 2 * q + core)
        c.start()
        ag.append(c)
    c = remote(gath.at[mine], gath.at[mine], fwd_send.at[chip], ag_recv.at[mine], partner)
    c.start()
    ag.append(c)
    u_forwards = [remote(ubuf.at[q], ubuf.at[q], uf_send.at[q], u_recv.at[q], partner) for q in sources]

    @pl.when(core == 1)
    def _():
        for c in u_forwards:
            c.wait_recv()
            c.start()

    for q in sources:
        s = core * chips + q
        remote(gath.at[s], gath.at[s], ag_send.at[q], ag_recv.at[s], 2 * q + core).wait_recv()
        c = remote(gath.at[s], gath.at[s], fwd_send.at[q], ag_recv.at[s], partner)
        c.start()
        ag.append(c)

    def await_parity(which):
        for q in range(chips):
            s = which * chips + q
            remote(gath.at[s], gath.at[s], fwd_send.at[q], ag_recv.at[s], partner).wait_recv()

    loads[9].wait()
    loads[10].wait()
    main_width = main_gain.shape[0]
    width = out.shape[1]
    half = chips * per
    gain = main_gain[...].reshape(1, main_width)
    pad = pad_vector[...].astype(F32).reshape(1, main_width - width)
    pad_sum = jnp.sum(pad * pad, axis=1, keepdims=True)
    pad_gain = pad * gain[:, width:]

    def hidden(which):
        rows_in = gath[pl.ds(which * chips, chips)].reshape(half, width).astype(F32)
        if which == 0:
            spill = ubuf[pl.ds(0, chips - 1)].reshape(half - per, width).astype(F32)
            rows_in = rows_in + jnp.concatenate([jnp.zeros((per, width), F32), spill], axis=0)
        mean = (jnp.sum(rows_in * rows_in, axis=1, keepdims=True) + pad_sum) / main_width
        scale = lax.rsqrt(mean + EPSILON)
        nbuf[:, :width] = (rows_in * scale * gain[:, :width]).astype(BF16)
        nbuf[:, width:] = (scale * pad_gain).astype(BF16)
        act = nbuf[...]
        hbuf[which] = (silu(mm(act, w_gate[...])) * mm(act, w_up[...])).astype(BF16)

    loads[11].wait()
    loads[12].wait()

    @pl.when(core == 0)
    def _():
        await_parity(1)

    hidden(1)

    @pl.when(core == 1)
    def _():
        await_parity(0)

    @pl.when(core == 0)
    def _():
        for q in range(chips):
            remote(ubuf.at[q], ubuf.at[q], uf_send.at[q], u_recv.at[q], partner).wait_recv()

    hidden(0)
    before_me = ubuf[lax.rem(chip + chips - 1, chips)].astype(F32)
    own_rows = gath[mine].astype(F32) + jnp.where((core == 0) & (chip > 0), before_me, 0.0)
    loads[13].wait()
    part[...] = mm(hbuf[1 - core], w_down[...]).astype(BF16).reshape(chips, per, width)
    rs = []
    targets = [lax.rem(chip + off, chips) for off in range(1, chips)] + [chip]
    for q in targets:
        c = remote(part.at[q], pair.at[q], pair_send.at[q], pair_recv.at[q], partner)
        c.start()
        rs.append(c)
    own_part[...] = mm(hbuf[core], w_down[...]).reshape(chips, per, width)
    for i, q in enumerate(targets):
        remote(part.at[q], pair.at[q], pair_send.at[q], pair_recv.at[q], partner).wait_recv()
        csend[q] = (own_part[q] + pair[q].astype(F32)).astype(BF16)
        if i < chips - 1:
            c = remote(
                csend.at[q], crecv.at[chip], chip_send.at[q], chip_recv.at[chip], 2 * q + core
            )
            c.start()
            rs.append(c)
    result = own_rows + csend[chip].astype(F32)
    for off in range(1, chips):
        q = lax.rem(chip + chips - off, chips)
        remote(csend.at[q], crecv.at[q], chip_send.at[q], chip_recv.at[q], 2 * q + core).wait_recv()
        result = result + crecv[q].astype(F32)
    table[pl.ds(TILE, per), :] = result.astype(BF16)
    fol = remote(
        table.at[pl.ds(TILE, per)],
        table.at[pl.ds(TILE + per, per)],
        one_send.at[2],
        one_recv.at[2],
        prv,
    )
    fol.start()
    ear = remote(
        table.at[pl.ds(per, TILE)],
        table.at[pl.ds(0, TILE)],
        one_send.at[3],
        one_recv.at[3],
        nxt,
    )
    ear.start()
    fol.wait_recv()
    ear.wait_recv()
    expanded = mm(spread, table[...])
    out[...] = (enc[...].astype(F32) + expanded).astype(BF16)

    for c in [halo_copy, fol, ear] + dec_copies + st1 + st2 + ag + rs:
        c.wait_send()

    @pl.when(core == 0)
    def _():
        up_copy.wait_send()

    @pl.when(core == 1)
    def _():
        for c in u_copies + u_forwards:
            c.wait_send()


def per_device(
    n,
    features,
    gate_in,
    conv_weight,
    conv_bias,
    log_decay,
    step_size,
    gate_gain,
    w_out,
    boundaries,
    pad_vector,
    main_gain,
    w_gate,
    w_up,
    w_down,
):
    rows, channels = features.shape
    inner = gate_in.shape[1]
    width = w_out.shape[1]
    state_dim = (channels - inner) // 2
    piece = state_dim // n
    chips = n // 2
    per = boundaries.shape[0] // n
    half = chips * per
    vmem = pl.BlockSpec(memory_space=pltpu.VMEM)
    hbm = pl.BlockSpec(memory_space=pl.ANY)
    dma = pltpu.SemaphoreType.DMA
    args = (
        features,
        gate_in,
        conv_weight,
        conv_bias,
        log_decay.T,
        step_size.T,
        gate_gain,
        w_out,
        boundaries,
        pad_vector,
        main_gain,
        w_gate,
        w_up,
        w_down,
    )
    return pl.pallas_call(
        functools.partial(kernel, n, per),
        out_shape=pltpu.VMEM((rows, width), BF16),
        in_specs=[hbm] * len(args),
        out_specs=vmem,
        scratch_shapes=[
            *[pltpu.VMEM(a.shape, a.dtype) for a in args],
            pltpu.VMEM((TILE, channels), BF16),
            pltpu.VMEM((TILE + rows, channels), F32),
            pltpu.VMEM((n, 8, 128), F32),
            pltpu.VMEM((n, piece, inner), BF16),
            pltpu.VMEM((n, piece, inner), BF16),
            pltpu.VMEM((n, piece, inner), BF16),
            pltpu.VMEM((n, piece, inner), BF16),
            pltpu.VMEM((rows, width), BF16),
            pltpu.VMEM((per, width), BF16),
            pltpu.VMEM((per, width), BF16),
            pltpu.VMEM((n, per, width), BF16),
            pltpu.VMEM((half, main_gain.shape[0]), BF16),
            pltpu.VMEM((chips, per, width), BF16),
            pltpu.VMEM((chips, per, width), BF16),
            pltpu.VMEM((chips, per, width), BF16),
            pltpu.VMEM((chips, per, width), BF16),
            pltpu.VMEM((chips, per, width), F32),
            pltpu.VMEM((chips, per, width), BF16),
            pltpu.VMEM((2, half, w_down.shape[0]), BF16),
            pltpu.VMEM((rows, inner), BF16),
            pltpu.VMEM((rows, 2 * state_dim), BF16),
            pltpu.VMEM((TILE + 2 * per, width), BF16),
            dma((len(args),)),
            dma((4,)),
            dma((4,)),
            dma((n,)),
            dma((n,)),
            dma((n,)),
            dma((n,)),
            dma((n,)),
            dma((n,)),
            dma((chips,)),
            dma((chips,)),
            dma((n,)),
            dma((chips,)),
            dma((chips,)),
            dma((chips,)),
            dma((chips,)),
            dma((chips,)),
            dma((chips,)),
            dma((chips,)),
        ],
        compiler_params=pltpu.CompilerParams(collective_id=0, has_side_effects=True),
    )(*args)


def solution(mesh):
    in_specs = (
        P(("doc", "seq"), None),
        P(("doc", "seq"), None),
        P(),
        P(),
        P(("doc", "seq"), None),
        P(("doc", "seq"), None),
        P(),
        P(),
        P("doc"),
        P(),
        P(),
        P(None, "seq"),
        P(None, "seq"),
        P("seq", None),
    )
    out_specs = P(("doc", "seq"), None)
    return jax.shard_map(
        functools.partial(per_device, mesh.shape["seq"]),
        mesh=mesh,
        in_specs=in_specs,
        out_specs=out_specs,
        check_vma=False,
    )
```
